32 devices in a mesh: rx: 16 (over z, y, core), shot: 2 (over x).
Axes of the slice: x: 2, y: 2, z: 4, core: 2. Of those that a mesh axis runs over, the one named last changes fastest.
Arguments:
- data: bfloat16 [3, 2, 4, 128, 128, 128], P(None, None, None, 'rx', 'shot'), may hold values from -6 to 6
- mixing: float32 [3, 2, 4, 4, 128, 128], P(None, None, None, None, 'rx'), may hold values from -3 to 3
- counts: int32 [3, 128], P(None, 'rx'), may hold values from 0 to 64
Outputs:
- fields: bfloat16 [3, 2, 4, 128, 128, 128], P(None, None, None, 'rx', 'shot')
- gram: float32 [3, 2, 128, 128, 128], P(None, None, 'rx', 'shot')
The draws below stay inside these ranges and needn't reach their ends.
All inputs are finite; a program needn't handle non-finite values.
Results may differ from the reference program's by a relative error of at most 0.0091.
Values may be sent and summed in bfloat16 or wider, within the bound.
A program may use at most 128 MiB of HBM per device.

```python
import math
import jax
import jax.numpy as jnp
from jax import lax

RX = 128
RY = 128
NF = 3
SHOTS_DEV = 64
SHOTS = 128


def set_ends(values, key, low, largest):
    longest = values.shape.index(max(values.shape))
    spots = []
    for shift in (0, 1):
        where = [jax.random.randint(jax.random.fold_in(key, axis), (), 0, length) for axis, length in enumerate(values.shape)]
        where[longest] = (where[longest] + shift) % values.shape[longest]
        spots.append(tuple(where))
    return values.at[spots[0]].set(low).at[spots[1]].set(largest)


def levels(stream_key, extent, pieces, least, high):
    gain, own = 1.0, jax.random.fold_in(stream_key, 6)
    for axis_at, parts in pieces:
        heights = jnp.exp(jax.random.uniform(jax.random.fold_in(own, axis_at), (parts,), jnp.float32, least / len(pieces), high / len(pieces)))
        gain = gain * jnp.repeat(heights, extent[axis_at] // parts).reshape([-1 if axis == axis_at else 1 for axis in range(len(extent))])
    return gain


def noise(own_key, extent, spread, bound, pieces=(), kind=jnp.bfloat16):
    values = jax.random.normal(own_key, extent, jnp.float32) * spread
    if len(pieces) > 0:
        values = levels(own_key, extent, pieces, -0.22, 0.18) * values
    return jnp.clip(values, min=-bound, max=bound).astype(kind)


def setup_inputs(seed: int = 0) -> dict:
    seeds = jax.random.split(jax.random.key(seed), 4)
    data = noise(seeds[0], (NF, 2, 4, RX, SHOTS, RY), 1.0, 6.0, ((3, 16), (4, 2)))
    mixing = noise(seeds[1], (NF, 2, 4, 4, RY, RX), 0.5, 3.0, ((4, 16),), jnp.float32)
    counts = set_ends(jax.random.randint(seeds[2], (NF, RY), 0, RX // 2 + 1), jax.random.fold_in(seeds[2], 1), 0, (RX // 2 + 1) - 1).astype(jnp.int32)
    return dict(data=data, mixing=mixing, counts=counts)


def dft_table(size, sign):
    steps = jnp.arange(size, dtype=jnp.int32)
    phases = steps[:, None] * steps[None, :] % size
    angles = phases.astype(jnp.float32) * (2.0 * math.pi / size)
    factor = 1.0 / math.sqrt(size)
    cosine = jnp.cos(angles) * factor
    sine = jnp.sin(angles) * (factor * sign)
    top_rows = jnp.stack([cosine, -sine], axis=1)
    low_rows = jnp.stack([sine, cosine], axis=1)
    return jnp.stack([top_rows, low_rows], axis=0).astype(jnp.bfloat16)

def apply_mix(matrix, values):
    return jnp.einsum('oikq,ikqs->okqs', matrix, values, precision=lax.Precision.HIGHEST)

def reference(data, mixing, counts):
    ry_forward = dft_table(RY, 1.0).astype(jnp.float32)
    rx_forward = dft_table(RX, 1.0).astype(jnp.float32)
    rx_inverse = dft_table(RX, -1.0).astype(jnp.float32)
    ry_inverse = dft_table(RY, -1.0).astype(jnp.float32)
    wave_index = jnp.arange(RX, dtype=jnp.int32)
    radial = jnp.minimum(wave_index, RX - wave_index)

    def one_bin(item):
        bin_data, bin_mix, bin_counts = item
        passing = (radial[None, :] <= bin_counts[:, None]).astype(jnp.float32)
        blocks = jnp.moveaxis(bin_data.reshape(2, 4, RX, SHOTS // SHOTS_DEV, SHOTS_DEV, RY), 3, 0)

        def one_block(total, block):
            spectra = jnp.einsum('cmxsy,cydk->dmkxs', block.astype(jnp.float32), ry_forward).astype(jnp.bfloat16)
            kspace = jnp.einsum('cmkxs,cxdq->dmkqs', spectra.astype(jnp.float32), rx_forward)
            mixed_real = apply_mix(bin_mix[0], kspace[0]) - apply_mix(bin_mix[1], kspace[1])
            mixed_imag = apply_mix(bin_mix[0], kspace[1]) + apply_mix(bin_mix[1], kspace[0])
            mixed = (jnp.stack([mixed_real, mixed_imag], axis=0) * passing[None, None, :, :, None]).astype(jnp.bfloat16)
            spaced = jnp.einsum('cmkqs,cqdx->dmkxs', mixed.astype(jnp.float32), rx_inverse).astype(jnp.bfloat16)
            downgo = spaced[:, 1].astype(jnp.float32)
            product = jnp.einsum('ckxs,dkzs->cdkxz', downgo, downgo)
            term = jnp.stack([product[0, 0] + product[1, 1], product[1, 0] - product[0, 1]], axis=0)
            fields = jnp.einsum('cmkxs,ckdy->dmxsy', spaced.astype(jnp.float32), ry_inverse).astype(jnp.bfloat16)
            return (total + term, fields)
        total, fields = lax.scan(one_block, jnp.zeros((2, RY, RX, RX), jnp.float32), blocks)
        fields = jnp.moveaxis(fields, 0, 3).reshape(2, 4, RX, SHOTS, RY)
        return (fields, total / SHOTS)
    fields, gram = lax.map(one_bin, (data, mixing, counts))
    return (fields, gram)
```

```python
import functools
import math

import jax
import jax.numpy as jnp
import numpy as np
from jax import lax
from jax.experimental import pallas as pl
from jax.experimental.pallas import tpu as pltpu
from jax.sharding import PartitionSpec as P

MESH = pl.DeviceIdType.MESH
NT = (((1,), (1,)), ((), ()))
TN = (((0,), (0,)), ((), ()))


def host_table(size, sign):
    steps = np.arange(size)
    angles = (steps[:, None] * steps[None, :] % size) * (2.0 * math.pi / size)
    factor = 1.0 / math.sqrt(size)
    cosine = np.cos(angles) * factor
    sine = np.sin(angles) * (factor * sign)
    table = np.stack(
        [np.stack([cosine, -sine], axis=1), np.stack([sine, cosine], axis=1)], axis=0
    )
    return table.astype(np.float32)


def flat(values):
    half = values.shape[0] * values.shape[1]
    return jnp.asarray(values.reshape(half, -1), jnp.bfloat16)


def tables(rx_size, ry_size, peers):
    lines = rx_size // peers
    ry_forward = host_table(ry_size, 1.0)
    rx_forward = host_table(rx_size, 1.0)
    rx_inverse = host_table(rx_size, -1.0)
    ry_inverse = host_table(ry_size, -1.0)
    first = flat(ry_forward.transpose(2, 3, 0, 1))
    split = rx_forward.reshape(2, peers, lines, 2, rx_size).transpose(1, 0, 2, 3, 4)
    second = jnp.asarray(split.reshape(2 * rx_size, 2 * rx_size), jnp.bfloat16)
    back = rx_inverse.transpose(2, 3, 0, 1)
    cut = back.reshape(2, peers, lines, 2, rx_size).transpose(1, 0, 2, 3, 4)
    third = jnp.asarray(cut.reshape(2 * rx_size, 2 * rx_size), jnp.bfloat16)
    whole = flat(back)
    fourth = flat(ry_inverse)
    return first, second, third, whole, fourth


def dot(left, right, dims):
    return lax.dot_general(left, right, dims, preferred_element_type=jnp.float32)


def kernel(
    peers, groups,
    data_ref, mixing_ref, passing_ref, t1, t2, t3, tg, t4,
    fields_ref, gram_ref,
    send1, recv1, send2, recv2, gbuf, stage, lift,
    out1_sem, in1_sem, out2_sem, in2_sem, gout_sem, gin_sem,
):
    bins, _, comps, lines, shots, ry_size = data_ref.shape
    waves = mixing_ref.shape[4]
    rx_size = mixing_ref.shape[5]
    pairs = comps // 2
    rows = 2 * lines
    me = lax.axis_index("rx")
    group = lax.axis_index("shot")
    others = sorted(range(1, peers), key=lambda o: abs(o - peers // 2))

    barrier = pltpu.get_barrier_semaphore()
    for offset in others:
        pl.semaphore_signal(
            barrier, inc=1, device_id=(lax.rem(me + offset, peers), group), device_id_type=MESH
        )
    for offset in range(1, groups):
        pl.semaphore_signal(
            barrier, inc=1, device_id=(me, lax.rem(group + offset, groups)), device_id_type=MESH
        )

    def forward_y(f, mp):
        def line(l, carry):
            parts = [
                jnp.concatenate(
                    [data_ref[f, c, 2 * mp, l], data_ref[f, c, 2 * mp + 1, l]], axis=0
                )
                for c in range(2)
            ]
            out = dot(t1[...], jnp.concatenate(parts, axis=1), NT)
            for d in range(2):
                stage[pl.ds(d * lines + l, ry_size, stride=rows), :] = out[
                    d * ry_size : (d + 1) * ry_size
                ]
            return carry

        for l in range(lines):
            line(l, 0)

        def pack(p, carry):
            size = waves * rows
            block = stage[pl.ds(pl.multiple_of(p * size, size), size), :]
            send1[f, mp, p] = block.reshape(waves, rows, 2 * shots).astype(jnp.bfloat16)
            return carry

        lax.fori_loop(0, peers, pack, 0)
        recv1[f, mp, me] = send1[f, mp, me]

    def send(source, target, f, mp, out_sem, in_sem):
        for offset in others:
            to = lax.rem(me + offset, peers)
            pltpu.make_async_remote_copy(
                src_ref=source.at[f, mp, to],
                dst_ref=target.at[f, mp, me],
                send_sem=out_sem.at[f, mp],
                recv_sem=in_sem.at[f, mp],
                device_id=(to, group),
                device_id_type=MESH,
            ).start()

    def await_all(buffer, f, mp, sem):
        part = buffer.at[f, mp, pl.ds(0, peers - 1)]
        pltpu.make_async_copy(part, part, sem.at[f, mp]).wait()

    def middle(f):
        def step(kp, carry):
            downs = []
            for k2 in range(2):
                k = 2 * kp + k2
                real, imag = [], []
                for mp in range(pairs):
                    seen = recv1[f, mp, :, k].reshape(2 * rx_size, 2 * shots)
                    ks = dot(seen, t2[...], TN)
                    for m2 in range(2):
                        real.append(ks[m2 * shots : (m2 + 1) * shots, :rx_size])
                        imag.append(ks[m2 * shots : (m2 + 1) * shots, rx_size:])
                mask = passing_ref[f, pl.ds(k, 1), :]
                mixed = []
                for o in range(comps):
                    total_r, total_i = None, None
                    for i in range(comps):
                        ar = mixing_ref[f, 0, o, i, pl.ds(k, 1), :]
                        ai = mixing_ref[f, 1, o, i, pl.ds(k, 1), :]
                        term_r = ar * real[i] - ai * imag[i]
                        term_i = ar * imag[i] + ai * real[i]
                        total_r = term_r if i == 0 else total_r + term_r
                        total_i = term_i if i == 0 else total_i + term_i
                    mixed.append(
                        jnp.concatenate([total_r * mask, total_i * mask], axis=1).astype(jnp.bfloat16)
                    )
                downs.append(mixed[1])
                for mp in range(pairs):
                    side = jnp.concatenate([mixed[2 * mp], mixed[2 * mp + 1]], axis=0)
                    out = dot(t3[...], side, NT).astype(jnp.bfloat16)
                    send2[f, mp, :, k] = out.reshape(peers, rows, 2 * shots)
            down = dot(tg[...], jnp.concatenate(downs, axis=0), NT)
            gbuf[group, f, kp] = down.astype(jnp.bfloat16)
            return carry

        lax.fori_loop(0, waves // 2, step, 0)
        for mp in range(pairs):
            recv2[f, mp, me] = send2[f, mp, me]

    def gram_send(f):
        for offset in range(1, groups):
            pltpu.make_async_remote_copy(
                src_ref=gbuf.at[group, f],
                dst_ref=gbuf.at[group, f],
                send_sem=gout_sem.at[f, offset],
                recv_sem=gin_sem.at[f, offset],
                device_id=(me, lax.rem(group + offset, groups)),
                device_id_type=MESH,
            ).start()

    def gram_wait(f):
        for offset in range(1, groups):
            part = gbuf.at[lax.rem(group + groups - offset, groups), f]
            pltpu.make_async_copy(part, part, gin_sem.at[f, offset]).wait()

    def gram(f):
        count = rx_size // groups
        first = pl.multiple_of(group * count, count)
        weight = 1.0 / (shots * groups)

        def step(kp, carry):
            for k2 in range(2):
                lanes = slice(k2 * shots, (k2 + 1) * shots)

                def take(start, size):
                    return jnp.concatenate(
                        [gbuf[j, f, kp, pl.ds(start, size), :][:, lanes] for j in range(groups)], axis=1
                    )

                real, imag = take(0, rx_size), take(rx_size, rx_size)
                mine = jnp.concatenate([take(first, count), take(rx_size + first, count)], axis=0)
                by_real, by_imag = dot(mine, real, NT), dot(mine, imag, NT)
                gram_ref[f, 0, 2 * kp + k2] = (by_real[:count] + by_imag[count:]) * weight
                gram_ref[f, 1, 2 * kp + k2] = (by_real[count:] - by_imag[:count]) * weight
            return carry

        lax.fori_loop(0, waves // 2, step, 0)

    def inverse_y(f, mp):
        def unpack(p, carry):
            size = waves * rows
            lift[pl.ds(pl.multiple_of(p * size, size), size), :] = (
                recv2[f, mp, p].reshape(size, 2 * shots).astype(jnp.float32)
            )
            return carry

        lax.fori_loop(0, peers, unpack, 0)
        for l in range(lines):
            left = jnp.concatenate(
                [lift[pl.ds(c * lines + l, ry_size, stride=rows), :] for c in range(2)], axis=0
            ).astype(jnp.bfloat16)
            out = dot(left, t4[...], TN).astype(jnp.bfloat16)
            for m2 in range(2):
                for d in range(2):
                    fields_ref[f, d, 2 * mp + m2, l] = out[
                        m2 * shots : (m2 + 1) * shots, d * ry_size : (d + 1) * ry_size
                    ]

    for f in range(bins):
        for mp in range(pairs):
            forward_y(f, mp)
            if f == 0 and mp == 0:
                pl.semaphore_wait(barrier, peers - 1 + groups - 1)
            send(send1, recv1, f, mp, out1_sem, in1_sem)
    for f in range(bins):
        for mp in range(pairs):
            await_all(recv1, f, mp, in1_sem)
        middle(f)
        for mp in range(pairs):
            send(send2, recv2, f, mp, out2_sem, in2_sem)
        gram_send(f)
        if f > 0:
            gram_wait(f - 1)
            gram(f - 1)
    gram_wait(bins - 1)
    gram(bins - 1)
    for f in range(bins):
        for mp in range(pairs):
            await_all(recv2, f, mp, in2_sem)
            inverse_y(f, mp)
    for f in range(bins):
        for mp in range(pairs):
            await_all(send1, f, mp, out1_sem)
            await_all(send2, f, mp, out2_sem)
        for offset in range(1, groups):
            part = gbuf.at[group, f]
            pltpu.make_async_copy(part, part, gout_sem.at[f, offset]).wait()


def fused(peers, groups, data, mixing, counts):
    bins, _, comps, lines, shots, ry_size = data.shape
    waves, rx_size = mixing.shape[4:]
    pairs = comps // 2
    wave_index = jnp.arange(rx_size, dtype=jnp.int32)
    radial = jnp.minimum(wave_index, rx_size - wave_index)
    passing = (radial[None, None, :] <= counts[:, :, None]).astype(jnp.float32)
    blocks = (bins, pairs, peers, waves, 2 * lines, 2 * shots)
    dma = pltpu.SemaphoreType.DMA
    vmem = pl.BlockSpec(memory_space=pltpu.VMEM)
    return pl.pallas_call(
        functools.partial(kernel, peers, groups),
        out_shape=(
            jax.ShapeDtypeStruct(data.shape, jnp.bfloat16),
            jax.ShapeDtypeStruct((bins, 2, waves, rx_size // groups, rx_size), jnp.float32),
        ),
        in_specs=[vmem] * 8,
        out_specs=(vmem, vmem),
        scratch_shapes=[pltpu.VMEM(blocks, jnp.bfloat16)] * 4
        + [
            pltpu.VMEM((groups, bins, waves // 2, 2 * rx_size, 2 * shots), jnp.bfloat16),
            pltpu.VMEM((ry_size * 2 * lines, 2 * shots), jnp.float32),
            pltpu.VMEM((ry_size * 2 * lines, 2 * shots), jnp.float32),
            dma((bins, pairs)), dma((bins, pairs)), dma((bins, pairs)), dma((bins, pairs)),
            dma((bins, groups)), dma((bins, groups)),
        ],
        compiler_params=pltpu.CompilerParams(
            collective_id=0, has_side_effects=True, vmem_limit_bytes=60 * 1024 * 1024
        ),
    )(data, mixing, passing, *tables(rx_size, ry_size, peers))


def dft_table(size, sign):
    steps = jnp.arange(size, dtype=jnp.int32)
    phases = steps[:, None] * steps[None, :] % size
    angles = phases.astype(jnp.float32) * (2.0 * math.pi / size)
    factor = 1.0 / math.sqrt(size)
    cosine = jnp.cos(angles) * factor
    sine = jnp.sin(angles) * (factor * sign)
    top_rows = jnp.stack([cosine, -sine], axis=1)
    low_rows = jnp.stack([sine, cosine], axis=1)
    return jnp.stack([top_rows, low_rows], axis=0).astype(jnp.bfloat16)


def apply_mix(matrix, values):
    return jnp.einsum("foikq,fikqs->fokqs", matrix, values, precision=lax.Precision.HIGHEST)


def per_device(data, mixing, counts):
    rx_size = mixing.shape[5]
    ry_size = data.shape[5]
    shots_here = data.shape[4]
    bin_count = data.shape[0]
    ry_forward = dft_table(ry_size, 1.0)
    rx_forward = dft_table(rx_size, 1.0)
    rx_inverse = dft_table(rx_size, -1.0)
    ry_inverse = dft_table(ry_size, -1.0)
    spectra = jnp.einsum(
        "fcmlsy,cydk->fdmkls", data, ry_forward, preferred_element_type=jnp.float32
    ).astype(jnp.bfloat16)
    pencils = jnp.stack(
        [
            lax.all_to_all(spectra[number], "rx", split_axis=2, concat_axis=3, tiled=True)
            for number in range(bin_count)
        ],
        axis=0,
    )
    kspace = jnp.einsum(
        "fcmkxs,cxdq->fdmkqs", pencils, rx_forward, preferred_element_type=jnp.float32
    )
    wave_index = jnp.arange(rx_size, dtype=jnp.int32)
    radial = jnp.minimum(wave_index, rx_size - wave_index)
    passing = (radial[None, None, :] <= counts[:, :, None]).astype(jnp.float32)
    mixed_real = apply_mix(mixing[:, 0], kspace[:, 0]) - apply_mix(mixing[:, 1], kspace[:, 1])
    mixed_imag = apply_mix(mixing[:, 0], kspace[:, 1]) + apply_mix(mixing[:, 1], kspace[:, 0])
    mixed = (
        jnp.stack([mixed_real, mixed_imag], axis=1) * passing[:, None, None, :, :, None]
    ).astype(jnp.bfloat16)
    spaced = jnp.einsum(
        "fcmkqs,cqdx->fdmkxs", mixed, rx_inverse, preferred_element_type=jnp.float32
    ).astype(jnp.bfloat16)
    downgo = spaced[:, :, 1]
    weight = 1.0 / (shots_here * lax.axis_size("shot"))
    row_count = rx_size // lax.axis_size("shot")
    first_row = lax.axis_index("shot") * row_count
    piece = lax.all_gather(downgo, "shot", axis=4, tiled=True)
    product = jnp.einsum(
        "fckxs,fdkzs->xfcdkz",
        lax.dynamic_slice_in_dim(piece, first_row, row_count, 3),
        piece,
        preferred_element_type=jnp.float32,
    )
    gram_rows = (
        jnp.stack(
            [product[:, :, 0, 0] + product[:, :, 1, 1], product[:, :, 1, 0] - product[:, :, 0, 1]],
            axis=2,
        )
        * weight
    )
    gram = jnp.transpose(gram_rows, (1, 2, 3, 0, 4))
    returned = jnp.stack(
        [
            lax.all_to_all(spaced[number], "rx", split_axis=3, concat_axis=2, tiled=True)
            for number in range(bin_count)
        ],
        axis=0,
    )
    fields = jnp.einsum(
        "fcmkls,ckdy->fdmlsy", returned, ry_inverse, preferred_element_type=jnp.float32
    ).astype(jnp.bfloat16)
    return (fields, gram)


def solution(mesh):
    peers, groups = mesh.shape["rx"], mesh.shape["shot"]

    def device_part(data, mixing, counts):
        _, _, comps, lines, shots, _ = data.shape
        waves = mixing.shape[4]
        if lines % 8 == 0 and shots % 64 == 0 and waves % 2 == 0 and comps % 2 == 0:
            return fused(peers, groups, data, mixing, counts)
        return per_device(data, mixing, counts)

    placed = (
        P(None, None, None, "rx", "shot", None),
        P(None, None, None, None, "rx", None),
        P(None, "rx"),
    )
    return jax.shard_map(
        device_part,
        mesh=mesh,
        in_specs=placed,
        out_specs=(P(None, None, None, "rx", "shot", None), P(None, None, "rx", "shot", None)),
        check_vma=False,
    )
```

```python
import functools
import math

import jax
import jax.numpy as jnp
import numpy as np
from jax import lax
from jax.experimental import pallas as pl
from jax.experimental.pallas import tpu as pltpu
from jax.sharding import PartitionSpec as P

MESH = pl.DeviceIdType.MESH
NT = (((1,), (1,)), ((), ()))
TN = (((0,), (0,)), ((), ()))


def host_table(size, sign):
    steps = np.arange(size)
    angles = (steps[:, None] * steps[None, :] % size) * (2.0 * math.pi / size)
    factor = 1.0 / math.sqrt(size)
    cosine = np.cos(angles) * factor
    sine = np.sin(angles) * (factor * sign)
    table = np.stack(
        [np.stack([cosine, -sine], axis=1), np.stack([sine, cosine], axis=1)], axis=0
    )
    return table.astype(np.float32)


def flat(values):
    half = values.shape[0] * values.shape[1]
    return jnp.asarray(values.reshape(half, -1), jnp.bfloat16)


def tables(rx_size, ry_size, peers):
    lines = rx_size // peers
    ry_forward = host_table(ry_size, 1.0)
    rx_forward = host_table(rx_size, 1.0)
    rx_inverse = host_table(rx_size, -1.0)
    ry_inverse = host_table(ry_size, -1.0)
    first = flat(ry_forward.transpose(2, 3, 0, 1))
    split = rx_forward.reshape(2, peers, lines, 2, rx_size).transpose(1, 0, 2, 3, 4)
    second = jnp.asarray(split.reshape(2 * rx_size, 2 * rx_size), jnp.bfloat16)
    back = rx_inverse.transpose(2, 3, 0, 1)
    cut = back.reshape(2, peers, lines, 2, rx_size).transpose(1, 0, 2, 3, 4)
    third = jnp.asarray(cut.reshape(2 * rx_size, 2 * rx_size), jnp.bfloat16)
    whole = flat(back)
    fourth = flat(ry_inverse)
    return first, second, third, whole, fourth


def dot(left, right, dims):
    return lax.dot_general(left, right, dims, preferred_element_type=jnp.float32)


def kernel(
    peers, groups,
    counts_ref, data_hbm, mixing_hbm, t1_hbm, t2_hbm, t3_hbm, tg_hbm, t4_hbm,
    fields_ref, gram_ref,
    data_ref, mixing_ref, t1, t2, t3, tg, t4,
    send1, recv1, send2, recv2, gbuf, stage, lift,
    out1_sem, in1_sem, out2_sem, in2_sem, gout_sem, gin_sem, load_sem, data_sem,
):
    bins, _, comps, lines, shots, ry_size = data_ref.shape
    waves = mixing_ref.shape[4]
    rx_size = mixing_ref.shape[5]
    pairs = comps // 2
    rows = 2 * lines
    me = lax.axis_index("rx")
    group = lax.axis_index("shot")
    others = sorted(range(1, peers), key=lambda o: abs(o - peers // 2))

    def load_data(f, mp):
        span = (f, slice(None), pl.ds(2 * mp, 2))
        return pltpu.make_async_copy(data_hbm.at[span], data_ref.at[span], data_sem.at[f, mp])

    loads = [
        pltpu.make_async_copy(source, target, load_sem.at[number])
        for number, (source, target) in enumerate(
            [(t1_hbm, t1), (t2_hbm, t2), (t3_hbm, t3), (tg_hbm, tg), (t4_hbm, t4), (mixing_hbm, mixing_ref)]
        )
    ]
    load_data(0, 0).start()
    loads[0].start()

    barrier = pltpu.get_barrier_semaphore()
    for offset in others:
        pl.semaphore_signal(
            barrier, inc=1, device_id=(lax.rem(me + offset, peers), group), device_id_type=MESH
        )
    for offset in range(1, groups):
        pl.semaphore_signal(
            barrier, inc=1, device_id=(me, lax.rem(group + offset, groups)), device_id_type=MESH
        )

    for f in range(bins):
        for mp in range(pairs):
            if f + mp > 0:
                load_data(f, mp).start()
    for load in loads[1:]:
        load.start()
    wave_index = lax.broadcasted_iota(jnp.int32, (1, rx_size), 1)
    radial = jnp.minimum(wave_index, rx_size - wave_index)

    def forward_y(f, mp):
        def line(l, carry):
            parts = [
                jnp.concatenate(
                    [data_ref[f, c, 2 * mp, l], data_ref[f, c, 2 * mp + 1, l]], axis=0
                )
                for c in range(2)
            ]
            out = dot(t1[...], jnp.concatenate(parts, axis=1), NT)
            for d in range(2):
                stage[pl.ds(d * lines + l, ry_size, stride=rows), :] = out[
                    d * ry_size : (d + 1) * ry_size
                ]
            return carry

        for l in range(lines):
            line(l, 0)

        if f == 0 and mp == 0:
            pl.semaphore_wait(barrier, peers - 1 + groups - 1)
        size = waves * rows

        def packed(p):
            block = stage[pl.ds(pl.multiple_of(p * size, size), size), :]
            return block.reshape(waves, rows, 2 * shots).astype(jnp.bfloat16)

        for offset in others:
            to = lax.rem(me + offset, peers)
            send1[f, mp, to] = packed(to)
            copy_to(send1, recv1, f, mp, out1_sem, in1_sem, to)
        recv1[f, mp, me] = packed(me)

    def copy_to(source, target, f, mp, out_sem, in_sem, to):
        pltpu.make_async_remote_copy(
            src_ref=source.at[f, mp, to],
            dst_ref=target.at[f, mp, me],
            send_sem=out_sem.at[f, mp],
            recv_sem=in_sem.at[f, mp],
            device_id=(to, group),
            device_id_type=MESH,
        ).start()

    def await_all(buffer, f, mp, sem):
        part = buffer.at[f, mp, pl.ds(0, peers - 1)]
        pltpu.make_async_copy(part, part, sem.at[f, mp]).wait()

    def middle(f):
        def step(kp, carry):
            downs = []
            for k2 in range(2):
                k = 2 * kp + k2
                real, imag = [], []
                for mp in range(pairs):
                    seen = recv1[f, mp, :, k].reshape(2 * rx_size, 2 * shots)
                    ks = dot(seen, t2[...], TN)
                    for m2 in range(2):
                        real.append(ks[m2 * shots : (m2 + 1) * shots, :rx_size])
                        imag.append(ks[m2 * shots : (m2 + 1) * shots, rx_size:])
                mask = jnp.where(radial <= counts_ref[f, k], 1.0, 0.0)
                mixed = []
                for o in range(comps):
                    total_r, total_i = None, None
                    for i in range(comps):
                        ar = mixing_ref[f, 0, o, i, pl.ds(k, 1), :]
                        ai = mixing_ref[f, 1, o, i, pl.ds(k, 1), :]
                        term_r = ar * real[i] - ai * imag[i]
                        term_i = ar * imag[i] + ai * real[i]
                        total_r = term_r if i == 0 else total_r + term_r
                        total_i = term_i if i == 0 else total_i + term_i
                    mixed.append(
                        jnp.concatenate([total_r * mask, total_i * mask], axis=1).astype(jnp.bfloat16)
                    )
                downs.append(mixed[1])
                for mp in range(pairs):
                    side = jnp.concatenate([mixed[2 * mp], mixed[2 * mp + 1]], axis=0)
                    out = dot(t3[...], side, NT).astype(jnp.bfloat16)
                    send2[f, mp, :, k] = out.reshape(peers, rows, 2 * shots)
            down = dot(tg[...], jnp.concatenate(downs, axis=0), NT)
            gbuf[group, f, kp] = down.astype(jnp.bfloat16)
            return carry

        lax.fori_loop(0, waves // 2, step, 0)
        for mp in range(pairs):
            recv2[f, mp, me] = send2[f, mp, me]

    def gram_send(f):
        for offset in range(1, groups):
            pltpu.make_async_remote_copy(
                src_ref=gbuf.at[group, f],
                dst_ref=gbuf.at[group, f],
                send_sem=gout_sem.at[f, offset],
                recv_sem=gin_sem.at[f, offset],
                device_id=(me, lax.rem(group + offset, groups)),
                device_id_type=MESH,
            ).start()

    def gram_wait(f):
        for offset in range(1, groups):
            part = gbuf.at[lax.rem(group + groups - offset, groups), f]
            pltpu.make_async_copy(part, part, gin_sem.at[f, offset]).wait()

    def gram(f):
        count = rx_size // groups
        first = pl.multiple_of(group * count, count)
        weight = 1.0 / (shots * groups)

        def step(kp, carry):
            for k2 in range(2):
                lanes = slice(k2 * shots, (k2 + 1) * shots)

                def take(start, size):
                    return jnp.concatenate(
                        [gbuf[j, f, kp, pl.ds(start, size), :][:, lanes] for j in range(groups)], axis=1
                    )

                real, imag = take(0, rx_size), take(rx_size, rx_size)
                mine = jnp.concatenate([take(first, count), take(rx_size + first, count)], axis=0)
                by_real, by_imag = dot(mine, real, NT), dot(mine, imag, NT)
                gram_ref[f, 0, 2 * kp + k2] = (by_real[:count] + by_imag[count:]) * weight
                gram_ref[f, 1, 2 * kp + k2] = (by_real[count:] - by_imag[:count]) * weight
            return carry

        lax.fori_loop(0, waves // 2, step, 0)

    def inverse_y(f, mp):
        def unpack(p, carry):
            size = waves * rows
            lift[pl.ds(pl.multiple_of(p * size, size), size), :] = (
                recv2[f, mp, p].reshape(size, 2 * shots).astype(jnp.float32)
            )
            return carry

        lax.fori_loop(0, peers, unpack, 0)
        for l in range(lines):
            left = jnp.concatenate(
                [lift[pl.ds(c * lines + l, ry_size, stride=rows), :] for c in range(2)], axis=0
            ).astype(jnp.bfloat16)
            out = dot(left, t4[...], TN).astype(jnp.bfloat16)
            for m2 in range(2):
                for d in range(2):
                    fields_ref[f, d, 2 * mp + m2, l] = out[
                        m2 * shots : (m2 + 1) * shots, d * ry_size : (d + 1) * ry_size
                    ]

    for f in range(bins):
        for mp in range(pairs):
            load_data(f, mp).wait()
            if f == 0 and mp == 0:
                loads[0].wait()
            forward_y(f, mp)
    for load in loads[1:]:
        load.wait()
    for f in range(bins):
        for mp in range(pairs):
            await_all(recv1, f, mp, in1_sem)
        middle(f)
        for mp in range(pairs):
            for offset in others:
                copy_to(send2, recv2, f, mp, out2_sem, in2_sem, lax.rem(me + offset, peers))
        gram_send(f)
        if f > 0:
            gram_wait(f - 1)
            gram(f - 1)
    gram_wait(bins - 1)
    gram(bins - 1)
    for f in range(bins):
        for mp in range(pairs):
            await_all(recv2, f, mp, in2_sem)
            inverse_y(f, mp)
    for f in range(bins):
        for mp in range(pairs):
            await_all(send1, f, mp, out1_sem)
            await_all(send2, f, mp, out2_sem)
        for offset in range(1, groups):
            part = gbuf.at[group, f]
            pltpu.make_async_copy(part, part, gout_sem.at[f, offset]).wait()


def fused(peers, groups, data, mixing, counts):
    bins, _, comps, lines, shots, ry_size = data.shape
    waves, rx_size = mixing.shape[4:]
    pairs = comps // 2
    blocks = (bins, pairs, peers, waves, 2 * lines, 2 * shots)
    dma = pltpu.SemaphoreType.DMA
    results = 2 * math.prod(data.shape) + 8 * bins * waves * rx_size * rx_size // groups
    vmem = pl.BlockSpec(memory_space=pltpu.VMEM)
    hbm = pl.BlockSpec(memory_space=pltpu.HBM)
    table = pltpu.VMEM((2 * rx_size, 2 * rx_size), jnp.bfloat16)
    table_y = pltpu.VMEM((2 * ry_size, 2 * ry_size), jnp.bfloat16)
    return pl.pallas_call(
        functools.partial(kernel, peers, groups),
        out_shape=(
            pltpu.VMEM(data.shape, jnp.bfloat16),
            pltpu.VMEM((bins, 2, waves, rx_size // groups, rx_size), jnp.float32),
        ),
        in_specs=[pl.BlockSpec(memory_space=pltpu.SMEM)] + [hbm] * 7,
        out_specs=(vmem, vmem),
        scratch_shapes=[
            pltpu.VMEM(data.shape, jnp.bfloat16),
            pltpu.VMEM(mixing.shape, jnp.float32),
            table_y, table, table, table, table_y,
        ]
        + [pltpu.VMEM(blocks, jnp.bfloat16)] * 4
        + [
            pltpu.VMEM((groups, bins, waves // 2, 2 * rx_size, 2 * shots), jnp.bfloat16),
            pltpu.VMEM((ry_size * 2 * lines, 2 * shots), jnp.float32),
            pltpu.VMEM((ry_size * 2 * lines, 2 * shots), jnp.float32),
            dma((bins, pairs)), dma((bins, pairs)), dma((bins, pairs)), dma((bins, pairs)),
            dma((bins, groups)), dma((bins, groups)), dma((6,)), dma((bins, pairs)),
        ],
        compiler_params=pltpu.CompilerParams(
            collective_id=0, has_side_effects=True, vmem_limit_bytes=67043328 - results - 131072
        ),
    )(counts, data, mixing, *tables(rx_size, ry_size, peers))


def dft_table(size, sign):
    steps = jnp.arange(size, dtype=jnp.int32)
    phases = steps[:, None] * steps[None, :] % size
    angles = phases.astype(jnp.float32) * (2.0 * math.pi / size)
    factor = 1.0 / math.sqrt(size)
    cosine = jnp.cos(angles) * factor
    sine = jnp.sin(angles) * (factor * sign)
    top_rows = jnp.stack([cosine, -sine], axis=1)
    low_rows = jnp.stack([sine, cosine], axis=1)
    return jnp.stack([top_rows, low_rows], axis=0).astype(jnp.bfloat16)


def apply_mix(matrix, values):
    return jnp.einsum("foikq,fikqs->fokqs", matrix, values, precision=lax.Precision.HIGHEST)


def per_device(data, mixing, counts):
    rx_size = mixing.shape[5]
    ry_size = data.shape[5]
    shots_here = data.shape[4]
    bin_count = data.shape[0]
    ry_forward = dft_table(ry_size, 1.0)
    rx_forward = dft_table(rx_size, 1.0)
    rx_inverse = dft_table(rx_size, -1.0)
    ry_inverse = dft_table(ry_size, -1.0)
    spectra = jnp.einsum(
        "fcmlsy,cydk->fdmkls", data, ry_forward, preferred_element_type=jnp.float32
    ).astype(jnp.bfloat16)
    pencils = jnp.stack(
        [
            lax.all_to_all(spectra[number], "rx", split_axis=2, concat_axis=3, tiled=True)
            for number in range(bin_count)
        ],
        axis=0,
    )
    kspace = jnp.einsum(
        "fcmkxs,cxdq->fdmkqs", pencils, rx_forward, preferred_element_type=jnp.float32
    )
    wave_index = jnp.arange(rx_size, dtype=jnp.int32)
    radial = jnp.minimum(wave_index, rx_size - wave_index)
    passing = (radial[None, None, :] <= counts[:, :, None]).astype(jnp.float32)
    mixed_real = apply_mix(mixing[:, 0], kspace[:, 0]) - apply_mix(mixing[:, 1], kspace[:, 1])
    mixed_imag = apply_mix(mixing[:, 0], kspace[:, 1]) + apply_mix(mixing[:, 1], kspace[:, 0])
    mixed = (
        jnp.stack([mixed_real, mixed_imag], axis=1) * passing[:, None, None, :, :, None]
    ).astype(jnp.bfloat16)
    spaced = jnp.einsum(
        "fcmkqs,cqdx->fdmkxs", mixed, rx_inverse, preferred_element_type=jnp.float32
    ).astype(jnp.bfloat16)
    downgo = spaced[:, :, 1]
    weight = 1.0 / (shots_here * lax.axis_size("shot"))
    row_count = rx_size // lax.axis_size("shot")
    first_row = lax.axis_index("shot") * row_count
    piece = lax.all_gather(downgo, "shot", axis=4, tiled=True)
    product = jnp.einsum(
        "fckxs,fdkzs->xfcdkz",
        lax.dynamic_slice_in_dim(piece, first_row, row_count, 3),
        piece,
        preferred_element_type=jnp.float32,
    )
    gram_rows = (
        jnp.stack(
            [product[:, :, 0, 0] + product[:, :, 1, 1], product[:, :, 1, 0] - product[:, :, 0, 1]],
            axis=2,
        )
        * weight
    )
    gram = jnp.transpose(gram_rows, (1, 2, 3, 0, 4))
    returned = jnp.stack(
        [
            lax.all_to_all(spaced[number], "rx", split_axis=3, concat_axis=2, tiled=True)
            for number in range(bin_count)
        ],
        axis=0,
    )
    fields = jnp.einsum(
        "fcmkls,ckdy->fdmlsy", returned, ry_inverse, preferred_element_type=jnp.float32
    ).astype(jnp.bfloat16)
    return (fields, gram)


def solution(mesh):
    peers, groups = mesh.shape["rx"], mesh.shape["shot"]

    def device_part(data, mixing, counts):
        _, _, comps, lines, shots, _ = data.shape
        waves = mixing.shape[4]
        if lines % 8 == 0 and shots % 64 == 0 and waves % 2 == 0 and comps % 2 == 0:
            return fused(peers, groups, data, mixing, counts)
        return per_device(data, mixing, counts)

    placed = (
        P(None, None, None, "rx", "shot", None),
        P(None, None, None, None, "rx", None),
        P(None, "rx"),
    )
    return jax.shard_map(
        device_part,
        mesh=mesh,
        in_specs=placed,
        out_specs=(P(None, None, None, "rx", "shot", None), P(None, None, "rx", "shot", None)),
        check_vma=False,
    )
```

```python
import functools
import math

import jax
import jax.numpy as jnp
import numpy as np
from jax import lax
from jax.experimental import pallas as pl
from jax.experimental.pallas import tpu as pltpu
from jax.sharding import PartitionSpec as P

MESH = pl.DeviceIdType.MESH
NT = (((1,), (1,)), ((), ()))
TN = (((0,), (0,)), ((), ()))


def host_table(size, sign):
    steps = np.arange(size)
    angles = (steps[:, None] * steps[None, :] % size) * (2.0 * math.pi / size)
    factor = 1.0 / math.sqrt(size)
    cosine = np.cos(angles) * factor
    sine = np.sin(angles) * (factor * sign)
    table = np.stack(
        [np.stack([cosine, -sine], axis=1), np.stack([sine, cosine], axis=1)], axis=0
    )
    return table.astype(np.float32)


def flat(values):
    half = values.shape[0] * values.shape[1]
    return jnp.asarray(values.reshape(half, -1), jnp.bfloat16)


def tables(rx_size, ry_size, peers):
    lines = rx_size // peers
    ry_forward = host_table(ry_size, 1.0)
    rx_forward = host_table(rx_size, 1.0)
    rx_inverse = host_table(rx_size, -1.0)
    ry_inverse = host_table(ry_size, -1.0)
    first = flat(ry_forward.transpose(2, 3, 0, 1))
    split = rx_forward.reshape(2, peers, lines, 2, rx_size).transpose(1, 0, 2, 3, 4)
    second = jnp.asarray(split.reshape(2 * rx_size, 2 * rx_size), jnp.bfloat16)
    back = rx_inverse.transpose(2, 3, 0, 1)
    cut = back.reshape(2, peers, lines, 2, rx_size).transpose(1, 0, 2, 3, 4)
    third = jnp.asarray(cut.reshape(2 * rx_size, 2 * rx_size), jnp.bfloat16)
    whole = flat(back)
    fourth = flat(ry_inverse)
    return first, second, third, whole, fourth


def dot(left, right, dims):
    return lax.dot_general(left, right, dims, preferred_element_type=jnp.float32)


def inverse_y(peers, seen, lift, table, put):
    _, waves, rows, lanes = seen.shape
    lines, shots, ry_size = rows // 2, lanes // 2, peers * waves
    size = waves * rows

    def unpack(p, carry):
        lift[pl.ds(pl.multiple_of(p * size, size), size), :] = (
            seen[p].reshape(size, lanes).astype(jnp.float32)
        )
        return carry

    lax.fori_loop(0, peers, unpack, 0)
    for l in range(lines):
        left = jnp.concatenate(
            [lift[pl.ds(c * lines + l, ry_size, stride=rows), :] for c in range(2)], axis=0
        ).astype(jnp.bfloat16)
        out = dot(left, table[...], TN).astype(jnp.bfloat16)
        for m2 in range(2):
            for d in range(2):
                put(d, m2, l, out[m2 * shots : (m2 + 1) * shots, d * ry_size : (d + 1) * ry_size])


def finish(peers, fields_ref, gram_ref, last_ref, t4, out_fields, out_gram, lift, tail, sem):
    bins, comps = fields_ref.shape[0], fields_ref.shape[2]
    end = bins - 1
    done = [pltpu.make_async_copy(gram_ref, out_gram, sem.at[bins])]
    for f in range(bins):
        span = (f,) if f < end else (f, slice(None), pl.ds(0, comps - 2))
        done.append(pltpu.make_async_copy(fields_ref.at[span], out_fields.at[span], sem.at[f]))
    for copy in done:
        copy.start()

    def put(d, m2, l, value):
        tail[d, m2, l] = value

    inverse_y(peers, last_ref, lift, t4, put)
    done.append(
        pltpu.make_async_copy(
            tail, out_fields.at[end, :, pl.ds(comps - 2, 2)], sem.at[bins + 1]
        )
    )
    done[-1].start()
    for copy in done:
        copy.wait()


def kernel(
    peers, groups,
    counts_ref, data_hbm, mixing_hbm, t1_hbm, t2_hbm, t3_hbm, tg_hbm, t4_hbm,
    fields_ref, gram_ref, last_ref,
    data_ref, mixing_ref, t1, t2, t3, tg, t4,
    send1, recv1, send2, recv2, gbuf, stage, lift,
    out1_sem, in1_sem, out2_sem, in2_sem, gout_sem, gin_sem, load_sem, data_sem,
):
    bins, _, comps, lines, shots, ry_size = data_ref.shape
    waves = mixing_ref.shape[4]
    rx_size = mixing_ref.shape[5]
    pairs = comps // 2
    rows = 2 * lines
    me = lax.axis_index("rx")
    group = lax.axis_index("shot")
    others = sorted(range(1, peers), key=lambda o: abs(o - peers // 2))

    def load_data(f, mp):
        span = (f, slice(None), pl.ds(2 * mp, 2))
        return pltpu.make_async_copy(data_hbm.at[span], data_ref.at[span], data_sem.at[f, mp])

    loads = [
        pltpu.make_async_copy(source, target, load_sem.at[number])
        for number, (source, target) in enumerate(
            [(t1_hbm, t1), (t2_hbm, t2), (t3_hbm, t3), (tg_hbm, tg), (t4_hbm, t4), (mixing_hbm, mixing_ref)]
        )
    ]
    load_data(0, 0).start()
    loads[0].start()

    barrier = pltpu.get_barrier_semaphore()
    for offset in others:
        pl.semaphore_signal(
            barrier, inc=1, device_id=(lax.rem(me + offset, peers), group), device_id_type=MESH
        )
    for offset in range(1, groups):
        pl.semaphore_signal(
            barrier, inc=1, device_id=(me, lax.rem(group + offset, groups)), device_id_type=MESH
        )

    for f in range(bins):
        for mp in range(pairs):
            if f + mp > 0:
                load_data(f, mp).start()
    for load in loads[1:]:
        load.start()
    wave_index = lax.broadcasted_iota(jnp.int32, (1, rx_size), 1)
    radial = jnp.minimum(wave_index, rx_size - wave_index)

    def forward_y(f, mp):
        def line(l, carry):
            parts = [
                jnp.concatenate(
                    [data_ref[f, c, 2 * mp, l], data_ref[f, c, 2 * mp + 1, l]], axis=0
                )
                for c in range(2)
            ]
            out = dot(t1[...], jnp.concatenate(parts, axis=1), NT)
            for d in range(2):
                stage[pl.ds(d * lines + l, ry_size, stride=rows), :] = out[
                    d * ry_size : (d + 1) * ry_size
                ]
            return carry

        for l in range(lines):
            line(l, 0)

        if f == 0 and mp == 0:
            pl.semaphore_wait(barrier, peers - 1 + groups - 1)
        size = waves * rows

        def packed(p):
            block = stage[pl.ds(pl.multiple_of(p * size, size), size), :]
            return block.reshape(waves, rows, 2 * shots).astype(jnp.bfloat16)

        for offset in others:
            to = lax.rem(me + offset, peers)
            send1[f, mp, to] = packed(to)
            copy_to(send1, recv1.at[f, mp], f, mp, out1_sem, in1_sem, to)
        recv1[f, mp, me] = packed(me)

    def copy_to(source, target, f, mp, out_sem, in_sem, to):
        pltpu.make_async_remote_copy(
            src_ref=source.at[f, mp, to],
            dst_ref=target.at[me],
            send_sem=out_sem.at[f, mp],
            recv_sem=in_sem.at[f, mp],
            device_id=(to, group),
            device_id_type=MESH,
        ).start()

    def await_all(buffer, f, mp, sem):
        part = buffer.at[f, mp, pl.ds(0, peers - 1)]
        pltpu.make_async_copy(part, part, sem.at[f, mp]).wait()

    def middle(f):
        def step(kp, carry):
            downs = []
            for k2 in range(2):
                k = 2 * kp + k2
                real, imag = [], []
                for mp in range(pairs):
                    seen = recv1[f, mp, :, k].reshape(2 * rx_size, 2 * shots)
                    ks = dot(seen, t2[...], TN)
                    for m2 in range(2):
                        real.append(ks[m2 * shots : (m2 + 1) * shots, :rx_size])
                        imag.append(ks[m2 * shots : (m2 + 1) * shots, rx_size:])
                mask = jnp.where(radial <= counts_ref[f, k], 1.0, 0.0)
                mixed = []
                for o in range(comps):
                    total_r, total_i = None, None
                    for i in range(comps):
                        ar = mixing_ref[f, 0, o, i, pl.ds(k, 1), :]
                        ai = mixing_ref[f, 1, o, i, pl.ds(k, 1), :]
                        term_r = ar * real[i] - ai * imag[i]
                        term_i = ar * imag[i] + ai * real[i]
                        total_r = term_r if i == 0 else total_r + term_r
                        total_i = term_i if i == 0 else total_i + term_i
                    mixed.append(
                        jnp.concatenate([total_r * mask, total_i * mask], axis=1).astype(jnp.bfloat16)
                    )
                downs.append(mixed[1])
                for mp in range(pairs):
                    side = jnp.concatenate([mixed[2 * mp], mixed[2 * mp + 1]], axis=0)
                    out = dot(t3[...], side, NT).astype(jnp.bfloat16)
                    send2[f, mp, :, k] = out.reshape(peers, rows, 2 * shots)
            down = dot(tg[...], jnp.concatenate(downs, axis=0), NT)
            gbuf[group, f, kp] = down.astype(jnp.bfloat16)
            return carry

        lax.fori_loop(0, waves // 2, step, 0)
        for mp in range(pairs):
            box2(f, mp)[me] = send2[f, mp, me]

    def gram_send(f):
        for offset in range(1, groups):
            pltpu.make_async_remote_copy(
                src_ref=gbuf.at[group, f],
                dst_ref=gbuf.at[group, f],
                send_sem=gout_sem.at[f, offset],
                recv_sem=gin_sem.at[f, offset],
                device_id=(me, lax.rem(group + offset, groups)),
                device_id_type=MESH,
            ).start()

    def gram_wait(f):
        for offset in range(1, groups):
            part = gbuf.at[lax.rem(group + groups - offset, groups), f]
            pltpu.make_async_copy(part, part, gin_sem.at[f, offset]).wait()

    def gram(f):
        count = rx_size // groups
        first = pl.multiple_of(group * count, count)
        weight = 1.0 / (shots * groups)

        def step(kp, carry):
            for k2 in range(2):
                lanes = slice(k2 * shots, (k2 + 1) * shots)

                def take(start, size):
                    return jnp.concatenate(
                        [gbuf[j, f, kp, pl.ds(start, size), :][:, lanes] for j in range(groups)], axis=1
                    )

                real, imag = take(0, rx_size), take(rx_size, rx_size)
                mine = jnp.concatenate([take(first, count), take(rx_size + first, count)], axis=0)
                by_real, by_imag = dot(mine, real, NT), dot(mine, imag, NT)
                gram_ref[f, 0, 2 * kp + k2] = (by_real[:count] + by_imag[count:]) * weight
                gram_ref[f, 1, 2 * kp + k2] = (by_real[count:] - by_imag[:count]) * weight
            return carry

        lax.fori_loop(0, waves // 2, step, 0)

    def box2(f, mp):
        return last_ref if (f, mp) == (bins - 1, pairs - 1) else recv2.at[f, mp]

    for f in range(bins):
        for mp in range(pairs):
            load_data(f, mp).wait()
            if f == 0 and mp == 0:
                loads[0].wait()
            forward_y(f, mp)
    for load in loads[1:]:
        load.wait()
    for f in range(bins):
        for mp in range(pairs):
            await_all(recv1, f, mp, in1_sem)
        middle(f)
        for mp in range(pairs):
            for offset in others:
                copy_to(send2, box2(f, mp), f, mp, out2_sem, in2_sem, lax.rem(me + offset, peers))
        gram_send(f)
        if f > 0:
            gram_wait(f - 1)
            gram(f - 1)
    gram_wait(bins - 1)
    gram(bins - 1)
    for f in range(bins):
        for mp in range(pairs):
            await_all(recv2, f, mp, in2_sem)
            if (f, mp) != (bins - 1, pairs - 1):

                def put(d, m2, l, value):
                    fields_ref[f, d, 2 * mp + m2, l] = value

                inverse_y(peers, box2(f, mp), lift, t4, put)
    for f in range(bins):
        for mp in range(pairs):
            await_all(send1, f, mp, out1_sem)
            await_all(send2, f, mp, out2_sem)
        for offset in range(1, groups):
            part = gbuf.at[group, f]
            pltpu.make_async_copy(part, part, gout_sem.at[f, offset]).wait()


def fused(peers, groups, data, mixing, counts):
    bins, _, comps, lines, shots, ry_size = data.shape
    waves, rx_size = mixing.shape[4:]
    pairs = comps // 2
    blocks = (bins, pairs, peers, waves, 2 * lines, 2 * shots)
    dma = pltpu.SemaphoreType.DMA
    gram_shape = (bins, 2, waves, rx_size // groups, rx_size)
    results = 2 * math.prod(data.shape) + 4 * math.prod(gram_shape) + 2 * math.prod(blocks[2:])
    vmem = pl.BlockSpec(memory_space=pltpu.VMEM)
    hbm = pl.BlockSpec(memory_space=pltpu.HBM)
    table = pltpu.VMEM((2 * rx_size, 2 * rx_size), jnp.bfloat16)
    table_y = pltpu.VMEM((2 * ry_size, 2 * ry_size), jnp.bfloat16)
    all_tables = tables(rx_size, ry_size, peers)
    fields, gram, last = pl.pallas_call(
        functools.partial(kernel, peers, groups),
        out_shape=(
            pltpu.VMEM(data.shape, jnp.bfloat16),
            pltpu.VMEM(gram_shape, jnp.float32),
            pltpu.VMEM(blocks[2:], jnp.bfloat16),
        ),
        in_specs=[pl.BlockSpec(memory_space=pltpu.SMEM)] + [hbm] * 7,
        out_specs=(vmem, vmem, vmem),
        scratch_shapes=[
            pltpu.VMEM(data.shape, jnp.bfloat16),
            pltpu.VMEM(mixing.shape, jnp.float32),
            table_y, table, table, table, table_y,
        ]
        + [pltpu.VMEM(blocks, jnp.bfloat16)] * 4
        + [
            pltpu.VMEM((groups, bins, waves // 2, 2 * rx_size, 2 * shots), jnp.bfloat16),
            pltpu.VMEM(((ry_size + 1) * 2 * lines, 2 * shots), jnp.float32),
            pltpu.VMEM(((ry_size + 1) * 2 * lines, 2 * shots), jnp.float32),
            dma((bins, pairs)), dma((bins, pairs)), dma((bins, pairs)), dma((bins, pairs)),
            dma((bins, groups)), dma((bins, groups)), dma((6,)), dma((bins, pairs)),
        ],
        compiler_params=pltpu.CompilerParams(
            collective_id=0, has_side_effects=True, vmem_limit_bytes=67043328 - results - 131072
        ),
    )(counts, data, mixing, *all_tables)
    anywhere = pl.BlockSpec(memory_space=pl.ANY)
    return pl.pallas_call(
        functools.partial(finish, peers),
        out_shape=(
            jax.ShapeDtypeStruct(fields.shape, fields.dtype),
            jax.ShapeDtypeStruct(gram.shape, gram.dtype),
        ),
        in_specs=[anywhere, anywhere, vmem, vmem],
        out_specs=(hbm, hbm),
        scratch_shapes=[
            pltpu.VMEM(((ry_size + 1) * 2 * lines, 2 * shots), jnp.float32),
            pltpu.VMEM((2, 2, lines, shots, ry_size), jnp.bfloat16),
            dma((bins + 2,)),
        ],
        compiler_params=pltpu.CompilerParams(vmem_limit_bytes=8 * 1024 * 1024),
    )(fields, gram, last, all_tables[4])


def dft_table(size, sign):
    steps = jnp.arange(size, dtype=jnp.int32)
    phases = steps[:, None] * steps[None, :] % size
    angles = phases.astype(jnp.float32) * (2.0 * math.pi / size)
    factor = 1.0 / math.sqrt(size)
    cosine = jnp.cos(angles) * factor
    sine = jnp.sin(angles) * (factor * sign)
    top_rows = jnp.stack([cosine, -sine], axis=1)
    low_rows = jnp.stack([sine, cosine], axis=1)
    return jnp.stack([top_rows, low_rows], axis=0).astype(jnp.bfloat16)


def apply_mix(matrix, values):
    return jnp.einsum("foikq,fikqs->fokqs", matrix, values, precision=lax.Precision.HIGHEST)


def per_device(data, mixing, counts):
    rx_size = mixing.shape[5]
    ry_size = data.shape[5]
    shots_here = data.shape[4]
    bin_count = data.shape[0]
    ry_forward = dft_table(ry_size, 1.0)
    rx_forward = dft_table(rx_size, 1.0)
    rx_inverse = dft_table(rx_size, -1.0)
    ry_inverse = dft_table(ry_size, -1.0)
    spectra = jnp.einsum(
        "fcmlsy,cydk->fdmkls", data, ry_forward, preferred_element_type=jnp.float32
    ).astype(jnp.bfloat16)
    pencils = jnp.stack(
        [
            lax.all_to_all(spectra[number], "rx", split_axis=2, concat_axis=3, tiled=True)
            for number in range(bin_count)
        ],
        axis=0,
    )
    kspace = jnp.einsum(
        "fcmkxs,cxdq->fdmkqs", pencils, rx_forward, preferred_element_type=jnp.float32
    )
    wave_index = jnp.arange(rx_size, dtype=jnp.int32)
    radial = jnp.minimum(wave_index, rx_size - wave_index)
    passing = (radial[None, None, :] <= counts[:, :, None]).astype(jnp.float32)
    mixed_real = apply_mix(mixing[:, 0], kspace[:, 0]) - apply_mix(mixing[:, 1], kspace[:, 1])
    mixed_imag = apply_mix(mixing[:, 0], kspace[:, 1]) + apply_mix(mixing[:, 1], kspace[:, 0])
    mixed = (
        jnp.stack([mixed_real, mixed_imag], axis=1) * passing[:, None, None, :, :, None]
    ).astype(jnp.bfloat16)
    spaced = jnp.einsum(
        "fcmkqs,cqdx->fdmkxs", mixed, rx_inverse, preferred_element_type=jnp.float32
    ).astype(jnp.bfloat16)
    downgo = spaced[:, :, 1]
    weight = 1.0 / (shots_here * lax.axis_size("shot"))
    row_count = rx_size // lax.axis_size("shot")
    first_row = lax.axis_index("shot") * row_count
    piece = lax.all_gather(downgo, "shot", axis=4, tiled=True)
    product = jnp.einsum(
        "fckxs,fdkzs->xfcdkz",
        lax.dynamic_slice_in_dim(piece, first_row, row_count, 3),
        piece,
        preferred_element_type=jnp.float32,
    )
    gram_rows = (
        jnp.stack(
            [product[:, :, 0, 0] + product[:, :, 1, 1], product[:, :, 1, 0] - product[:, :, 0, 1]],
            axis=2,
        )
        * weight
    )
    gram = jnp.transpose(gram_rows, (1, 2, 3, 0, 4))
    returned = jnp.stack(
        [
            lax.all_to_all(spaced[number], "rx", split_axis=3, concat_axis=2, tiled=True)
            for number in range(bin_count)
        ],
        axis=0,
    )
    fields = jnp.einsum(
        "fcmkls,ckdy->fdmlsy", returned, ry_inverse, preferred_element_type=jnp.float32
    ).astype(jnp.bfloat16)
    return (fields, gram)


def solution(mesh):
    peers, groups = mesh.shape["rx"], mesh.shape["shot"]

    def device_part(data, mixing, counts):
        _, _, comps, lines, shots, _ = data.shape
        waves = mixing.shape[4]
        if lines % 8 == 0 and shots % 64 == 0 and waves % 2 == 0 and comps % 2 == 0:
            return fused(peers, groups, data, mixing, counts)
        return per_device(data, mixing, counts)

    placed = (
        P(None, None, None, "rx", "shot", None),
        P(None, None, None, None, "rx", None),
        P(None, "rx"),
    )
    return jax.shard_map(
        device_part,
        mesh=mesh,
        in_specs=placed,
        out_specs=(P(None, None, None, "rx", "shot", None), P(None, None, "rx", "shot", None)),
        check_vma=False,
    )
```
